128 devices in a mesh: gx: 8 (over y, core), gy: 16 (over x, z).
Axes of the slice: x: 4, y: 4, z: 4, core: 2. Of those that a mesh axis runs over, the one named last changes fastest.
Arguments:
- near_tiles: bfloat16 [8, 16, 32, 20, 128, 128], P('gx', 'gy'), may hold values from -0.125 to 0.125
- block: bfloat16 [8, 16, 4096, 64], P('gx', 'gy'), may hold values from -7 to 7, as said below
- adjacency: int32 [8, 16, 32, 20], P('gx', 'gy'), may hold values from 0 to 4095, as said below
Outputs:
- basis: float32 [8, 16, 4096, 64], P('gx', 'gy')
- r_factor: float32 [64, 64], replicated
The draws below stay inside these ranges and needn't reach their ends.
Inputs may be any that keep to these rules, and one draw needn't show every extreme that they name: `adjacency`: entry 0 of each row tile is the row tile itself; every entry names a tile of the device of its row tile or of a device whose gx and gy indices each differ by at most one, without wrapping. `block`: entries are real values of order one, within -7 to 7.
All inputs are finite; a program needn't handle non-finite values.
Results may differ from the reference program's by a relative error of at most 0.0003.
Values may be sent and summed in bfloat16 or wider, within the bound.
A program may use at most 128 MiB of HBM per device.

```python
import jax
import jax.numpy as jnp
from jax import lax

K = 64
TILE = 128
NB = 20
TILES_DEV = 32
ROWS_DEV = 4096
ROWS = 524288
N_GX = 8
N_GY = 16


def draw_block(key, part):
    first, second, third = jax.random.split(jax.random.fold_in(key, 11), 3)
    shape = (N_GX, N_GY, ROWS_DEV, K)
    noise = jnp.clip(jax.random.normal(first, shape, jnp.float32), -4.0, 4.0)
    shared = jnp.clip(jax.random.normal(second, (N_GX, N_GY, ROWS_DEV, 1), jnp.float32), -4.0, 4.0)
    weights = jax.random.uniform(third, (K,), jnp.float32, 0.5, 1.5)
    return (0.7 * (noise + shared * weights)).astype(jnp.bfloat16)


def draw_adjacency(key, part):
    first, second, third = jax.random.split(jax.random.fold_in(key, 23), 3)
    shape = (N_GX, N_GY, TILES_DEV, NB)
    grid_x = lax.broadcasted_iota(jnp.int32, shape, 0)
    grid_y = lax.broadcasted_iota(jnp.int32, shape, 1)
    own_tile = lax.broadcasted_iota(jnp.int32, shape, 2)
    entry = lax.broadcasted_iota(jnp.int32, shape, 3)
    step_x = jax.random.randint(first, shape, -1, 2, jnp.int32)
    step_y = jax.random.randint(second, shape, -1, 2, jnp.int32)
    target_x = jnp.clip(grid_x + step_x, 0, N_GX - 1)
    target_y = jnp.clip(grid_y + step_y, 0, N_GY - 1)
    target_tile = jax.random.randint(third, shape, 0, TILES_DEV, jnp.int32)
    column = (target_x * N_GY + target_y) * TILES_DEV + target_tile
    diagonal = (grid_x * N_GY + grid_y) * TILES_DEV + own_tile
    return jnp.where(entry == 0, diagonal, column).astype(jnp.int32)


def steps_of(own_key, extent, cuts, smallest, high):
    loudness = 1.0
    for dim, shards_of in cuts:
        heights = jax.random.uniform(jax.random.fold_in(jax.random.fold_in(own_key, 6), dim), (shards_of,), jnp.float32, smallest / len(cuts), high / len(cuts))
        loudness = loudness * jnp.repeat(jnp.exp(heights), extent[dim] // shards_of).reshape((-1,) + (1,) * (len(extent) - 1 - dim))
    return loudness


def bell_draw(key, extent, spread, reach, cuts=(), kind=jnp.bfloat16):
    level = steps_of(key, extent, cuts, -0.22, 0.18) if cuts else 1.0
    array = jax.random.normal(key, extent, jnp.float32) * spread * level
    return jnp.minimum(jnp.maximum(array, -reach), reach).astype(kind)


def setup_inputs(seed: int = 0) -> dict:
    splits = jax.random.split(jax.random.key(seed), 4)
    return {
        "near_tiles": bell_draw(splits[0], (N_GX, N_GY, TILES_DEV, NB, TILE, TILE), (NB * TILE) ** -0.5, 0.125, ((0, 8), (1, 16))),
        "block": draw_block(jax.random.fold_in(splits[3], 71), 0),
        "adjacency": draw_adjacency(jax.random.fold_in(splits[3], 71), 0),
    }


def reference(near_tiles, block, adjacency):
    tiles_all = near_tiles.reshape(-1, NB, TILE, TILE)
    rows_all = block.reshape(-1, TILE, K)
    links = adjacency.reshape(-1, NB)

    def one_device(index):
        start = (index * TILES_DEV).astype(jnp.int32)
        tiles = lax.dynamic_slice_in_dim(tiles_all, start, TILES_DEV, 0).astype(jnp.float32)
        picks = lax.dynamic_slice_in_dim(links, start, TILES_DEV, 0)
        chosen = rows_all[picks].astype(jnp.float32)
        return jnp.einsum('rnij,rnjk->rik', tiles, chosen, precision=lax.Precision.HIGHEST)
    parts = lax.map(one_device, jnp.arange(N_GX * N_GY, dtype=jnp.int32))
    image = parts.reshape(-1, K)
    gram = jnp.dot(image.T, image, precision=lax.Precision.HIGHEST)
    upper = jnp.linalg.cholesky(gram).T
    ortho_t = jax.scipy.linalg.solve_triangular(upper.T, image.T, lower=True)
    scale = jnp.sqrt(jnp.float32(ROWS))
    basis = (ortho_t.T * scale).reshape(N_GX, N_GY, ROWS_DEV, K)
    return (basis, upper / scale)
```

```python
import functools

import jax
import jax.numpy as jnp
from jax import lax
from jax.experimental import pallas as pl
from jax.experimental.pallas import tpu as pltpu
from jax.sharding import PartitionSpec as P

K = 64
TILE = 128
NB = 20
TILES = 32
ROWS_DEV = TILES * TILE
N_GX = 8
N_GY = 16
ROWS = ROWS_DEV * N_GX * N_GY
CHUNKS = 4
PART = TILES // CHUNKS
A_COPIES = 8
UNROLL = 8
MESH = pl.DeviceIdType.MESH


def slot_of(x, y):
    return (lax.rem(x, 4) * 4 + lax.rem(y, 4)) * TILES


def folded(gram):
    rows = gram[:K] + gram[K:]
    both = rows + pltpu.roll(rows, K, 1)
    lane = lax.broadcasted_iota(jnp.int32, (K // 2, 2 * K), 1)
    return jnp.where(lane < K, both[: K // 2], both[K // 2 :])


def product_kernel(
    tiles_hbm, block_hbm, places, split_ref, gram_ref,
    tiles, table, turned, across_x, across_y,
    tile_sem, own_sem, gy_send, gy_recv, gx_send, gx_recv, sx_send, sx_recv, sy_send, sy_recv,
):
    me_x, me_y = lax.axis_index("gx"), lax.axis_index("gy")

    def ring_x(step):
        return lax.rem(me_x + step + N_GX, N_GX)

    def ring_y(step):
        return lax.rem(me_y + step + N_GY, N_GY)

    own = slot_of(me_x, me_y)
    own_copy = pltpu.make_async_copy(block_hbm, turned, own_sem)
    own_copy.start()

    barrier = pltpu.get_barrier_semaphore()
    for step in range(1, N_GX):
        pl.semaphore_signal(barrier, inc=1, device_id=(ring_x(step), me_y), device_id_type=MESH)
    for step in range(1, N_GY):
        pl.semaphore_signal(barrier, inc=1, device_id=(me_x, ring_y(step)), device_id_type=MESH)
    own_copy.wait()
    for i in range(TILES):
        table[own + i] = turned[:, i * TILE : (i + 1) * TILE]
    pl.semaphore_wait(barrier, N_GX + N_GY - 2)

    started = []

    def span(slot, part):
        return table.at[pl.ds(slot + part * PART, PART)]

    def push(slot, part, send, recv, device):
        copy = pltpu.make_async_remote_copy(
            src_ref=span(slot, part), dst_ref=span(slot, part), send_sem=send, recv_sem=recv,
            device_id=device, device_id_type=MESH,
        )
        copy.start()
        started.append(copy)

    def push_x(slot, which, part):
        for d, step in enumerate((1, -1)):
            push(slot, part, gx_send.at[d, which, part], gx_recv.at[d, which, part], (ring_x(step), me_y))

    for part in range(CHUNKS):
        for d, step in enumerate((1, -1)):
            push(own, part, gy_send.at[d, part], gy_recv.at[d, part], (me_x, ring_y(step)))
        push_x(own, 0, part)

    copies = []
    group = TILES // A_COPIES
    for i in range(A_COPIES):
        copy = pltpu.make_async_copy(
            tiles_hbm.at[pl.ds(i * group, group)], tiles.at[pl.ds(i * group, group)], tile_sem.at[i]
        )
        copy.start()
        copies.append(copy)

    def landed(slot, part, sem):
        pltpu.make_async_copy(span(slot, part), span(slot, part), sem).wait()

    for part in range(CHUNKS):
        for d, step in enumerate((-1, 1)):
            slot = slot_of(me_x, ring_y(step))
            landed(slot, part, gy_recv.at[d, part])
            push_x(slot, 1 + d, part)
    for copy in copies:
        copy.wait()
    for which, dy in enumerate((0, -1, 1)):
        for part in range(CHUNKS):
            for d, step in enumerate((-1, 1)):
                landed(slot_of(ring_x(step), ring_y(dy)), part, gx_recv.at[d, which, part])

    def row_tile(t, carry):
        near = jnp.concatenate([tiles[t, j] for j in range(NB)], axis=1)
        rows = jnp.concatenate([table[places[j, t]] for j in range(NB)], axis=1)
        image = lax.dot_general(
            near, rows, (((1,), (1,)), ((), ())), preferred_element_type=jnp.float32
        ).T
        high = image.astype(jnp.bfloat16)
        low = (image - high.astype(jnp.float32)).astype(jnp.bfloat16)
        here = pl.ds(pl.multiple_of(t * TILE, TILE), TILE)
        split_ref[:K, here] = high
        split_ref[K:, here] = low
        return carry

    lax.fori_loop(0, TILES, row_tile, 0, unroll=UNROLL)
    split = split_ref[...]
    gram = lax.dot_general(split, split, (((1,), (1,)), ((), ())), preferred_element_type=jnp.float32)

    def summed(value, gathered, count, me, send, recv, device):
        gathered[me] = value
        sends = []
        for step in range(1, count):
            copy = pltpu.make_async_remote_copy(
                src_ref=gathered.at[me], dst_ref=gathered.at[me], send_sem=send.at[step], recv_sem=recv.at[step],
                device_id=device(step), device_id_type=MESH,
            )
            copy.start()
            sends.append(copy)
        for step in range(1, count):
            source = gathered.at[lax.rem(me - step + count, count)]
            pltpu.make_async_copy(source, source, recv.at[step]).wait()
        terms = [gathered[i] for i in range(count)]
        while len(terms) > 1:
            terms = [a + b for a, b in zip(terms[::2], terms[1::2])]
        return terms[0], sends

    partial, sends_x = summed(
        folded(gram), across_x, N_GX, me_x, sx_send, sx_recv, lambda step: (ring_x(step), me_y)
    )
    total, sends_y = summed(
        partial, across_y, N_GY, me_y, sy_send, sy_recv, lambda step: (me_x, ring_y(step))
    )
    swapped = pltpu.roll(total, K, 1)
    lane = lax.broadcasted_iota(jnp.int32, total.shape, 1)
    gram_ref[: K // 2] = jnp.where(lane < K, total, swapped)
    gram_ref[K // 2 :] = jnp.where(lane < K, swapped, total)
    for copy in started + sends_x + sends_y:
        copy.wait_send()


def eliminated(rows):
    count = K // 8
    sub = lax.broadcasted_iota(jnp.int32, (8, 128), 0)
    zero = jnp.zeros((8, 128), jnp.float32)

    def spread(x):
        return jnp.broadcast_to(x, (8, 128))

    pivots = []
    for p in range(count):
        columns = [
            {r: spread(rows[r][:, 8 * p + j : 8 * p + j + 1]) for r in range(p, count)} for j in range(8)
        ]
        found = zero
        for j in range(8):
            pivot = spread(columns[j][p][j : j + 1])
            found = jnp.where(sub == j, pivot, found)
            inverse = 1.0 / pivot
            pivot_row = spread(rows[p][j : j + 1])
            later = {i: spread(columns[i][p][j : j + 1]) for i in range(j + 1, 8)}
            for r in range(p, count):
                scaled = columns[j][r] * inverse
                if r == p:
                    scaled = jnp.where(sub > j, scaled, zero)
                for i in range(j + 1, 8):
                    columns[i][r] = columns[i][r] - scaled * later[i]
                rows[r] = rows[r] - scaled * pivot_row
        pivots.append(found)
    return rows, pivots


BASIS_PARTS = 4


def basis_kernel(gram_ref, split_hbm, basis_hbm, factor_ref, split, basis, sems):
    fetch = pltpu.make_async_copy(split_hbm, split, sems.at[BASIS_PARTS])
    fetch.start()
    lane = lax.broadcasted_iota(jnp.int32, (8, 128), 1)
    sub = lax.broadcasted_iota(jnp.int32, (8, 128), 0)
    count = K // 8
    rows = [
        jnp.where(lane < K, gram_ref[8 * r : 8 * r + 8], jnp.where(lane - K == sub + 8 * r, 1.0, 0.0))
        for r in range(count)
    ]
    rows, pivots = eliminated(rows)
    scale = float(ROWS) ** 0.5
    highs, lows = [], []
    for r in range(count):
        root = lax.rsqrt(pivots[r])
        root = root * (1.5 - 0.5 * pivots[r] * root * root)
        upper = rows[r] * root
        factor_ref[8 * r : 8 * r + 8] = (jnp.where(lane >= sub + 8 * r, upper, 0.0) * (1.0 / scale))[:, :K]
        solve = upper * scale
        solve = jnp.where(lane < K, pltpu.roll(solve, K, 1), solve)
        high = solve.astype(jnp.bfloat16)
        highs.append(high)
        lows.append((solve - high.astype(jnp.float32)).astype(jnp.bfloat16))
    solver = jnp.concatenate([jnp.concatenate(highs, 0), jnp.concatenate(lows, 0)], 1)
    fetch.wait()
    width = ROWS_DEV // BASIS_PARTS
    stores = []
    for part in range(BASIS_PARTS):
        here = slice(part * width, (part + 1) * width)
        image = split[:, here]
        basis[:, here] = jnp.dot(solver, jnp.concatenate([image, image], 0), preferred_element_type=jnp.float32)
        at = pl.ds(part * width, width)
        store = pltpu.make_async_copy(basis.at[:, at], basis_hbm.at[:, at], sems.at[part])
        store.start()
        stores.append(store)
    for store in stores:
        store.wait()


def shards(near_tiles, block, adjacency):
    any_space, vmem, smem = (
        pl.BlockSpec(memory_space=space) for space in (pl.ANY, pltpu.VMEM, pltpu.SMEM)
    )
    dma = pltpu.SemaphoreType.DMA
    links = jnp.swapaxes(adjacency[0, 0], 0, 1)
    owner = links // TILES
    places = slot_of(owner // N_GY, owner % N_GY) + links % TILES
    split, gram = pl.pallas_call(
        product_kernel,
        name="near_product",
        out_shape=(
            jax.ShapeDtypeStruct((2 * K, ROWS_DEV), jnp.bfloat16),
            jax.ShapeDtypeStruct((K, 2 * K), jnp.float32),
        ),
        in_specs=[any_space, any_space, smem],
        out_specs=(vmem, vmem),
        scratch_shapes=[
            pltpu.VMEM((TILES, NB, TILE, TILE), jnp.bfloat16),
            pltpu.VMEM((16 * TILES, K, TILE), jnp.bfloat16),
            pltpu.VMEM((K, ROWS_DEV), jnp.bfloat16),
            pltpu.VMEM((N_GX, K // 2, 2 * K), jnp.float32),
            pltpu.VMEM((N_GY, K // 2, 2 * K), jnp.float32),
            dma((A_COPIES,)),
            dma,
            dma((2, CHUNKS)),
            dma((2, CHUNKS)),
            dma((2, 3, CHUNKS)),
            dma((2, 3, CHUNKS)),
            dma((N_GX,)),
            dma((N_GX,)),
            dma((N_GY,)),
            dma((N_GY,)),
        ],
        compiler_params=pltpu.CompilerParams(
            collective_id=0, has_side_effects=True, vmem_limit_bytes=56 * 1024 * 1024
        ),
    )(near_tiles[0, 0], jnp.swapaxes(block[0, 0], 0, 1), places)
    basis, factor = pl.pallas_call(
        basis_kernel,
        name="orthonormal_basis",
        out_shape=(
            jax.ShapeDtypeStruct((K, ROWS_DEV), jnp.float32),
            jax.ShapeDtypeStruct((K, K), jnp.float32),
        ),
        in_specs=[vmem, any_space],
        out_specs=(any_space, vmem),
        scratch_shapes=[
            pltpu.VMEM((2 * K, ROWS_DEV), jnp.bfloat16),
            pltpu.VMEM((K, ROWS_DEV), jnp.float32),
            dma((BASIS_PARTS + 1,)),
        ],
    )(gram, split)
    return (jnp.swapaxes(basis, 0, 1).reshape(1, 1, ROWS_DEV, K), factor)


def solution(mesh):
    in_specs = (
        P("gx", "gy", None, None, None, None),
        P("gx", "gy", None, None),
        P("gx", "gy", None, None),
    )
    out_specs = (P("gx", "gy", None, None), P())
    return jax.shard_map(shards, mesh=mesh, in_specs=in_specs, out_specs=out_specs, check_vma=False)
```

```python
import functools

import jax
import jax.numpy as jnp
from jax import lax
from jax.experimental import pallas as pl
from jax.experimental.pallas import tpu as pltpu
from jax.sharding import PartitionSpec as P

K = 64
TILE = 128
NB = 20
TILES = 32
ROWS_DEV = TILES * TILE
N_GX = 8
N_GY = 16
ROWS = ROWS_DEV * N_GX * N_GY
CHUNKS = 4
TURNED = 1
TURN_AT = 2
PART = TILES // CHUNKS
A_COPIES = 8
UNROLL = 8
MESH = pl.DeviceIdType.MESH


def slot_of(x, y):
    return (lax.rem(x, 4) * 4 + lax.rem(y, 4)) * TILES


def folded(gram):
    rows = gram[:K] + gram[K:]
    both = rows + pltpu.roll(rows, K, 1)
    lane = lax.broadcasted_iota(jnp.int32, (K // 2, 2 * K), 1)
    return jnp.where(lane < K, both[: K // 2], both[K // 2 :])


def product_kernel(
    tiles_hbm, block_hbm, links_hbm, split, gram_ref,
    tiles, table, turned, links, across_x, across_y,
    tile_sem, own_sem, gy_send, gy_recv, near_send, near_recv, far_send, far_recv, turn_send, turn_recv,
    sx_send, sx_recv, sy_send, sy_recv, links_sem,
):
    me_x, me_y = lax.axis_index("gx"), lax.axis_index("gy")

    def ring_x(step):
        return lax.rem(me_x + step + N_GX, N_GX)

    def ring_y(step):
        return lax.rem(me_y + step + N_GY, N_GY)

    core = lax.rem(me_x, 2)
    near_x = me_x + 1 - 2 * core
    far_x = ring_x(2 * core - 1)
    own = slot_of(me_x, me_y)

    barrier = pltpu.get_barrier_semaphore()

    def greet(x, y):
        pl.semaphore_signal(barrier, inc=1, device_id=(x, y), device_id_type=MESH)

    for step in sorted(range(1, N_GY), key=lambda n: min(n, N_GY - n)):
        greet(me_x, ring_y(step))
    for step in sorted(range(1, N_GX), key=lambda n: min(n, N_GX - n)):
        greet(ring_x(step), me_y)
    own_copy = pltpu.make_async_copy(block_hbm, turned, own_sem)
    own_copy.start()
    links_copy = pltpu.make_async_copy(links_hbm, links, links_sem)
    links_copy.start()
    own_copy.wait()
    for i in range(TILES):
        table[own + i] = turned[:, i * TILE : (i + 1) * TILE]
    pl.semaphore_wait(barrier, N_GX + N_GY - 2)

    started = []

    def span(slot, part):
        return table.at[pl.ds(slot + part * PART, PART)]

    def push(slot, part, send, recv, x, y):
        copy = pltpu.make_async_remote_copy(
            src_ref=span(slot, part), dst_ref=span(slot, part), send_sem=send, recv_sem=recv,
            device_id=(x, y), device_id_type=MESH,
        )
        copy.start()
        started.append(copy)

    def landed(slot, part, sem):
        pltpu.make_async_copy(span(slot, part), span(slot, part), sem).wait()

    for part in range(CHUNKS):
        for d, step in enumerate((1, -1)):
            push(own, part, gy_send.at[d, part], gy_recv.at[d, part], me_x, ring_y(step))
        push(own, part, far_send.at[0, part], far_recv.at[0, part], far_x, me_y)
        push(own, part, near_send.at[0, part], near_recv.at[0, part], near_x, me_y)

    copies = []
    group = TILES // A_COPIES
    for i in range(A_COPIES):
        copy = pltpu.make_async_copy(
            tiles_hbm.at[pl.ds(i * group, group)], tiles.at[pl.ds(i * group, group)], tile_sem.at[i]
        )
        copy.start()
        copies.append(copy)

    early = CHUNKS - TURNED
    for part in range(CHUNKS):
        for d, step in enumerate((-1, 1)):
            slot = slot_of(me_x, ring_y(step))
            landed(slot, part, gy_recv.at[d, part])
            if part < early:
                push(slot, part, far_send.at[1 + d, part], far_recv.at[1 + d, part], far_x, me_y)
            push(slot, part, near_send.at[1 + d, part], near_recv.at[1 + d, part], near_x, me_y)
        if part == TURN_AT:
            for late in range(TURNED):
                slot = slot_of(far_x, me_y)
                landed(slot, early + late, far_recv.at[0, early + late])
                for d, step in enumerate((1, -1)):
                    push(slot, early + late, turn_send.at[d, late], turn_recv.at[d, late], me_x, ring_y(step))
    links_copy.wait()
    for copy in copies:
        copy.wait()
    for which, dy in enumerate((0, -1, 1)):
        for part in range(CHUNKS):
            landed(slot_of(near_x, ring_y(dy)), part, near_recv.at[which, part])
            if part < early:
                landed(slot_of(far_x, ring_y(dy)), part, far_recv.at[which, part])
            elif which:
                landed(slot_of(far_x, ring_y(dy)), part, turn_recv.at[which - 1, part - early])

    def row_tile(t, carry):
        near = jnp.concatenate([tiles[t, j] for j in range(NB)], axis=1)
        picked = []
        for j in range(NB):
            link = links[j, 0, t]
            picked.append(table[((link >> 2) & (12 * TILES)) | (link & (4 * TILES - 1))])
        rows = jnp.concatenate(picked, axis=1)
        image = lax.dot_general(
            near, rows, (((1,), (1,)), ((), ())), preferred_element_type=jnp.float32
        ).T
        high = image.astype(jnp.bfloat16)
        low = (image - high.astype(jnp.float32)).astype(jnp.bfloat16)
        here = pl.ds(pl.multiple_of(t * TILE, TILE), TILE)
        split[:K, here] = high
        split[K:, here] = low
        return carry

    lax.fori_loop(0, TILES, row_tile, 0, unroll=UNROLL)
    image = split[...]
    gram = lax.dot_general(image, image, (((1,), (1,)), ((), ())), preferred_element_type=jnp.float32)

    def summed(value, gathered, count, me, send, recv, device):
        gathered[me] = value
        sends = []
        for step in range(1, count):
            copy = pltpu.make_async_remote_copy(
                src_ref=gathered.at[me], dst_ref=gathered.at[me], send_sem=send.at[step], recv_sem=recv.at[step],
                device_id=device(step), device_id_type=MESH,
            )
            copy.start()
            sends.append(copy)
        for step in range(1, count):
            source = gathered.at[lax.rem(me - step + count, count)]
            pltpu.make_async_copy(source, source, recv.at[step]).wait()
        terms = [gathered[i] for i in range(count)]
        while len(terms) > 1:
            terms = [a + b for a, b in zip(terms[::2], terms[1::2])]
        return terms[0], sends

    partial, sends_x = summed(
        folded(gram), across_x, N_GX, me_x, sx_send, sx_recv, lambda step: (ring_x(step), me_y)
    )
    total, sends_y = summed(
        partial, across_y, N_GY, me_y, sy_send, sy_recv, lambda step: (me_x, ring_y(step))
    )
    swapped = pltpu.roll(total, K, 1)
    lane = lax.broadcasted_iota(jnp.int32, total.shape, 1)
    gram_ref[: K // 2] = jnp.where(lane < K, total, swapped)
    gram_ref[K // 2 :] = jnp.where(lane < K, swapped, total)
    for copy in started + sends_x + sends_y:
        copy.wait_send()


def eliminated(rows):
    count = K // 8
    sub = lax.broadcasted_iota(jnp.int32, (8, 128), 0)
    zero = jnp.zeros((8, 128), jnp.float32)

    def spread(x):
        return jnp.broadcast_to(x, (8, 128))

    pivots = []
    for p in range(count):
        columns = [
            {r: spread(rows[r][:, 8 * p + j : 8 * p + j + 1]) for r in range(p, count)} for j in range(8)
        ]
        found = zero
        for j in range(8):
            pivot = spread(columns[j][p][j : j + 1])
            found = jnp.where(sub == j, pivot, found)
            inverse = 1.0 / pivot
            pivot_row = spread(rows[p][j : j + 1])
            later = {i: spread(columns[i][p][j : j + 1]) for i in range(j + 1, 8)}
            for r in range(p, count):
                scaled = columns[j][r] * inverse
                if r == p:
                    scaled = jnp.where(sub > j, scaled, zero)
                for i in range(j + 1, 8):
                    columns[i][r] = columns[i][r] - scaled * later[i]
                rows[r] = rows[r] - scaled * pivot_row
        pivots.append(found)
    return rows, pivots


BASIS_PARTS = 4


def basis_kernel(gram_ref, split, basis_hbm, factor_ref, basis, sems):
    lane = lax.broadcasted_iota(jnp.int32, (8, 128), 1)
    sub = lax.broadcasted_iota(jnp.int32, (8, 128), 0)
    count = K // 8
    rows = [
        jnp.where(lane < K, gram_ref[8 * r : 8 * r + 8], jnp.where(lane - K == sub + 8 * r, 1.0, 0.0))
        for r in range(count)
    ]
    rows, pivots = eliminated(rows)
    scale = float(ROWS) ** 0.5
    highs, lows = [], []
    for r in range(count):
        root = lax.rsqrt(pivots[r])
        root = root * (1.5 - 0.5 * pivots[r] * root * root)
        upper = rows[r] * root
        factor_ref[8 * r : 8 * r + 8] = (jnp.where(lane >= sub + 8 * r, upper, 0.0) * (1.0 / scale))[:, :K]
        solve = upper * scale
        solve = jnp.where(lane < K, pltpu.roll(solve, K, 1), solve)
        high = solve.astype(jnp.bfloat16)
        highs.append(high)
        lows.append((solve - high.astype(jnp.float32)).astype(jnp.bfloat16))
    solver = jnp.concatenate([jnp.concatenate(highs, 0), jnp.concatenate(lows, 0)], 1)
    width = ROWS_DEV // BASIS_PARTS
    stores = []
    for part in range(BASIS_PARTS):
        here = slice(part * width, (part + 1) * width)
        image = split[:, here]
        basis[:, here] = jnp.dot(solver, jnp.concatenate([image, image], 0), preferred_element_type=jnp.float32)
        at = pl.ds(part * width, width)
        store = pltpu.make_async_copy(basis.at[:, at], basis_hbm.at[:, at], sems.at[part])
        store.start()
        stores.append(store)
    for store in stores:
        store.wait()


def shards(near_tiles, block, adjacency):
    hbm, vmem = (pl.BlockSpec(memory_space=space) for space in (pltpu.HBM, pltpu.VMEM))
    dma = pltpu.SemaphoreType.DMA
    links = jnp.transpose(adjacency, (0, 3, 1, 2)).reshape(NB, 1, TILES)
    turned = jnp.swapaxes(block[0, 0], 0, 1)
    split, gram = pl.pallas_call(
        product_kernel,
        name="near_product",
        out_shape=(
            jax.ShapeDtypeStruct((2 * K, ROWS_DEV), jnp.bfloat16),
            jax.ShapeDtypeStruct((K, 2 * K), jnp.float32),
        ),
        in_specs=[hbm, hbm, hbm],
        out_specs=(vmem, vmem),
        scratch_shapes=[
            pltpu.VMEM((TILES, NB, TILE, TILE), jnp.bfloat16),
            pltpu.VMEM((16 * TILES, K, TILE), jnp.bfloat16),
            pltpu.VMEM((K, ROWS_DEV), jnp.bfloat16),
            pltpu.SMEM((NB, 1, TILES), jnp.int32),
            pltpu.VMEM((N_GX, K // 2, 2 * K), jnp.float32),
            pltpu.VMEM((N_GY, K // 2, 2 * K), jnp.float32),
            dma((A_COPIES,)),
            dma,
            dma((2, CHUNKS)),
            dma((2, CHUNKS)),
            dma((3, CHUNKS)),
            dma((3, CHUNKS)),
            dma((3, CHUNKS)),
            dma((3, CHUNKS)),
            dma((2, TURNED)),
            dma((2, TURNED)),
            dma((N_GX,)),
            dma((N_GX,)),
            dma((N_GY,)),
            dma((N_GY,)),
            dma,
        ],
        compiler_params=pltpu.CompilerParams(
            collective_id=0, has_side_effects=True, vmem_limit_bytes=40 * 1024 * 1024
        ),
    )(near_tiles[0, 0], *(pltpu.with_memory_space_constraint(x, pltpu.HBM) for x in (turned, links)))
    basis, factor = pl.pallas_call(
        basis_kernel,
        name="orthonormal_basis",
        out_shape=(
            jax.ShapeDtypeStruct((K, ROWS_DEV), jnp.float32),
            jax.ShapeDtypeStruct((K, K), jnp.float32),
        ),
        in_specs=[vmem, vmem],
        out_specs=(hbm, vmem),
        scratch_shapes=[
            pltpu.VMEM((K, ROWS_DEV), jnp.float32),
            dma((BASIS_PARTS,)),
        ],
        compiler_params=pltpu.CompilerParams(vmem_limit_bytes=8 * 1024 * 1024),
    )(gram, split)
    return (jnp.swapaxes(basis, 0, 1).reshape(1, 1, ROWS_DEV, K), factor)


def solution(mesh):
    in_specs = (
        P("gx", "gy", None, None, None, None),
        P("gx", "gy", None, None),
        P("gx", "gy", None, None),
    )
    out_specs = (P("gx", "gy", None, None), P())
    return jax.shard_map(shards, mesh=mesh, in_specs=in_specs, out_specs=out_specs, check_vma=False)
```

```python
import functools

import jax
import jax.numpy as jnp
from jax import lax
from jax.experimental import pallas as pl
from jax.experimental.pallas import tpu as pltpu
from jax.sharding import PartitionSpec as P

K = 64
TILE = 128
NB = 20
TILES = 32
ROWS_DEV = TILES * TILE
N_GX = 8
N_GY = 16
ROWS = ROWS_DEV * N_GX * N_GY
CHUNKS = 4
TURNED = 1
TURN_AT = 2
PART = TILES // CHUNKS
A_COPIES = 8
UNROLL = TILES
MESH = pl.DeviceIdType.MESH


def slot_of(x, y):
    return (lax.rem(x, 4) * 4 + lax.rem(y, 4)) * TILES


def folded(gram):
    rows = gram[:K] + gram[K:]
    both = rows + pltpu.roll(rows, K, 1)
    lane = lax.broadcasted_iota(jnp.int32, (K // 2, 2 * K), 1)
    return jnp.where(lane < K, both[: K // 2], both[K // 2 :])


def product_kernel(
    tiles_hbm, block_hbm, links_hbm, split, gram_ref,
    tiles, table, turned, links, across_x, across_y,
    tile_sem, own_sem, gy_send, gy_recv, near_send, near_recv, far_send, far_recv, turn_send, turn_recv,
    sx_send, sx_recv, sy_send, sy_recv, links_sem,
):
    me_x, me_y = lax.axis_index("gx"), lax.axis_index("gy")

    def ring_x(step):
        return lax.rem(me_x + step + N_GX, N_GX)

    def ring_y(step):
        return lax.rem(me_y + step + N_GY, N_GY)

    core = lax.rem(me_x, 2)
    near_x = me_x + 1 - 2 * core
    far_x = ring_x(2 * core - 1)
    own = slot_of(me_x, me_y)

    own_copy = pltpu.make_async_copy(block_hbm, turned, own_sem)
    own_copy.start()
    links_copy = pltpu.make_async_copy(links_hbm, links, links_sem)
    links_copy.start()
    barrier = pltpu.get_barrier_semaphore()

    def greet(x, y):
        pl.semaphore_signal(barrier, inc=1, device_id=(x, y), device_id_type=MESH)

    for step in sorted(range(1, N_GY), key=lambda n: min(n, N_GY - n)):
        greet(me_x, ring_y(step))
    for step in sorted(range(1, N_GX), key=lambda n: min(n, N_GX - n)):
        greet(ring_x(step), me_y)
    own_copy.wait()
    for i in range(TILES):
        table[own + i] = turned[:, i * TILE : (i + 1) * TILE]
    pl.semaphore_wait(barrier, N_GX + N_GY - 2)

    started = []

    def span(slot, part):
        return table.at[pl.ds(slot + part * PART, PART)]

    def push(slot, part, send, recv, x, y):
        copy = pltpu.make_async_remote_copy(
            src_ref=span(slot, part), dst_ref=span(slot, part), send_sem=send, recv_sem=recv,
            device_id=(x, y), device_id_type=MESH,
        )
        copy.start()
        started.append(copy)

    def landed(slot, part, sem):
        pltpu.make_async_copy(span(slot, part), span(slot, part), sem).wait()

    for part in range(CHUNKS):
        for d, step in enumerate((1, -1)):
            push(own, part, gy_send.at[d, part], gy_recv.at[d, part], me_x, ring_y(step))
        push(own, part, far_send.at[0, part], far_recv.at[0, part], far_x, me_y)
        push(own, part, near_send.at[0, part], near_recv.at[0, part], near_x, me_y)

    copies = []
    group = TILES // A_COPIES
    for i in range(A_COPIES):
        copy = pltpu.make_async_copy(
            tiles_hbm.at[pl.ds(i * group, group)], tiles.at[pl.ds(i * group, group)], tile_sem.at[i]
        )
        copy.start()
        copies.append(copy)

    early = CHUNKS - TURNED
    for part in range(CHUNKS):
        for d, step in enumerate((-1, 1)):
            slot = slot_of(me_x, ring_y(step))
            landed(slot, part, gy_recv.at[d, part])
            if part < early:
                push(slot, part, far_send.at[1 + d, part], far_recv.at[1 + d, part], far_x, me_y)
            push(slot, part, near_send.at[1 + d, part], near_recv.at[1 + d, part], near_x, me_y)
        if part == TURN_AT:
            for late in range(TURNED):
                slot = slot_of(far_x, me_y)
                landed(slot, early + late, far_recv.at[0, early + late])
                for d, step in enumerate((1, -1)):
                    push(slot, early + late, turn_send.at[d, late], turn_recv.at[d, late], me_x, ring_y(step))
    links_copy.wait()
    for copy in copies:
        copy.wait()
    for which, dy in enumerate((0, -1, 1)):
        for part in range(CHUNKS):
            landed(slot_of(near_x, ring_y(dy)), part, near_recv.at[which, part])
            if part < early:
                landed(slot_of(far_x, ring_y(dy)), part, far_recv.at[which, part])
            elif which:
                landed(slot_of(far_x, ring_y(dy)), part, turn_recv.at[which - 1, part - early])

    def row_tile(t, carry):
        near = jnp.concatenate([tiles[t, j] for j in range(NB)], axis=1)
        picked = []
        for j in range(NB):
            link = links[j, 0, t]
            picked.append(table[((link >> 2) & (12 * TILES)) | (link & (4 * TILES - 1))])
        rows = jnp.concatenate(picked, axis=1)
        image = lax.dot_general(
            near, rows, (((1,), (1,)), ((), ())), preferred_element_type=jnp.float32
        ).T
        high = image.astype(jnp.bfloat16)
        low = (image - high.astype(jnp.float32)).astype(jnp.bfloat16)
        here = pl.ds(pl.multiple_of(t * TILE, TILE), TILE)
        split[:K, here] = high
        split[K:, here] = low
        return carry

    lax.fori_loop(0, TILES, row_tile, 0, unroll=UNROLL)
    image = split[...]
    gram = lax.dot_general(image, image, (((1,), (1,)), ((), ())), preferred_element_type=jnp.float32)

    def summed(value, gathered, count, me, send, recv, device):
        gathered[me] = value
        sends = []
        for step in range(1, count):
            copy = pltpu.make_async_remote_copy(
                src_ref=gathered.at[me], dst_ref=gathered.at[me], send_sem=send.at[step], recv_sem=recv.at[step],
                device_id=device(step), device_id_type=MESH,
            )
            copy.start()
            sends.append(copy)
        for step in range(1, count):
            source = gathered.at[lax.rem(me - step + count, count)]
            pltpu.make_async_copy(source, source, recv.at[step]).wait()
        terms = [gathered[i] for i in range(count)]
        while len(terms) > 1:
            terms = [a + b for a, b in zip(terms[::2], terms[1::2])]
        return terms[0], sends

    partial, sends_x = summed(
        folded(gram), across_x, N_GX, me_x, sx_send, sx_recv, lambda step: (ring_x(step), me_y)
    )
    total, sends_y = summed(
        partial, across_y, N_GY, me_y, sy_send, sy_recv, lambda step: (me_x, ring_y(step))
    )
    swapped = pltpu.roll(total, K, 1)
    lane = lax.broadcasted_iota(jnp.int32, total.shape, 1)
    gram_ref[: K // 2] = jnp.where(lane < K, total, swapped)
    gram_ref[K // 2 :] = jnp.where(lane < K, swapped, total)
    for copy in started + sends_x + sends_y:
        copy.wait_send()


def eliminated(rows):
    count = K // 8
    sub = lax.broadcasted_iota(jnp.int32, (8, 128), 0)
    zero = jnp.zeros((8, 128), jnp.float32)

    def spread(x):
        return jnp.broadcast_to(x, (8, 128))

    pivots = [zero] * count
    for first in range(0, K, PANEL):
        columns = [
            {r: spread(rows[r][:, first + j : first + j + 1]) for r in range(first // 8, count)} for j in range(PANEL)
        ]
        for j in range(PANEL):
            p, at = divmod(first + j, 8)
            pivot = spread(columns[j][p][at : at + 1])
            pivots[p] = jnp.where(sub == at, pivot, pivots[p])
            inverse = 1.0 / pivot
            pivot_row = spread(rows[p][at : at + 1])
            later = {i: spread(columns[i][p][at : at + 1]) for i in range(j + 1, PANEL)}
            for r in range(p, count):
                scaled = columns[j][r] * inverse
                if r == p:
                    scaled = jnp.where(sub > at, scaled, zero)
                for i in range(j + 1, PANEL):
                    columns[i][r] = columns[i][r] - scaled * later[i]
                rows[r] = rows[r] - scaled * pivot_row
    return rows, pivots


PANEL = 16
BASIS_PARTS = 4


def basis_kernel(gram_ref, split, basis_hbm, factor_ref, basis, sems):
    lane = lax.broadcasted_iota(jnp.int32, (8, 128), 1)
    sub = lax.broadcasted_iota(jnp.int32, (8, 128), 0)
    count = K // 8
    rows = [
        jnp.where(lane < K, gram_ref[8 * r : 8 * r + 8], jnp.where(lane - K == sub + 8 * r, 1.0, 0.0))
        for r in range(count)
    ]
    rows, pivots = eliminated(rows)
    scale = float(ROWS) ** 0.5
    highs, lows = [], []
    for r in range(count):
        root = lax.rsqrt(pivots[r])
        root = root * (1.5 - 0.5 * pivots[r] * root * root)
        upper = rows[r] * root
        factor_ref[8 * r : 8 * r + 8] = (jnp.where(lane >= sub + 8 * r, upper, 0.0) * (1.0 / scale))[:, :K]
        solve = upper * scale
        solve = jnp.where(lane < K, pltpu.roll(solve, K, 1), solve)
        high = solve.astype(jnp.bfloat16)
        highs.append(high)
        lows.append((solve - high.astype(jnp.float32)).astype(jnp.bfloat16))
    solver = jnp.concatenate([jnp.concatenate(highs, 0), jnp.concatenate(lows, 0)], 1)
    width = ROWS_DEV // BASIS_PARTS
    stores = []
    for part in range(BASIS_PARTS):
        here = slice(part * width, (part + 1) * width)
        image = split[:, here]
        basis[:, here] = jnp.dot(solver, jnp.concatenate([image, image], 0), preferred_element_type=jnp.float32)
        at = pl.ds(part * width, width)
        store = pltpu.make_async_copy(basis.at[:, at], basis_hbm.at[:, at], sems.at[part])
        store.start()
        stores.append(store)
    for store in stores:
        store.wait()


def shards(near_tiles, block, adjacency):
    hbm, vmem = (pl.BlockSpec(memory_space=space) for space in (pltpu.HBM, pltpu.VMEM))
    dma = pltpu.SemaphoreType.DMA
    links = jnp.transpose(adjacency, (0, 3, 1, 2)).reshape(NB, 1, TILES)
    turned = jnp.swapaxes(block[0, 0], 0, 1)
    split, gram = pl.pallas_call(
        product_kernel,
        name="near_product",
        out_shape=(
            jax.ShapeDtypeStruct((2 * K, ROWS_DEV), jnp.bfloat16),
            jax.ShapeDtypeStruct((K, 2 * K), jnp.float32),
        ),
        in_specs=[hbm, hbm, hbm],
        out_specs=(vmem, vmem),
        scratch_shapes=[
            pltpu.VMEM((TILES, NB, TILE, TILE), jnp.bfloat16),
            pltpu.VMEM((16 * TILES, K, TILE), jnp.bfloat16),
            pltpu.VMEM((K, ROWS_DEV), jnp.bfloat16),
            pltpu.SMEM((NB, 1, TILES), jnp.int32),
            pltpu.VMEM((N_GX, K // 2, 2 * K), jnp.float32),
            pltpu.VMEM((N_GY, K // 2, 2 * K), jnp.float32),
            dma((A_COPIES,)),
            dma,
            dma((2, CHUNKS)),
            dma((2, CHUNKS)),
            dma((3, CHUNKS)),
            dma((3, CHUNKS)),
            dma((3, CHUNKS)),
            dma((3, CHUNKS)),
            dma((2, TURNED)),
            dma((2, TURNED)),
            dma((N_GX,)),
            dma((N_GX,)),
            dma((N_GY,)),
            dma((N_GY,)),
            dma,
        ],
        compiler_params=pltpu.CompilerParams(
            collective_id=0, has_side_effects=True, vmem_limit_bytes=40 * 1024 * 1024
        ),
    )(near_tiles[0, 0], *(pltpu.with_memory_space_constraint(x, pltpu.HBM) for x in (turned, links)))
    basis, factor = pl.pallas_call(
        basis_kernel,
        name="orthonormal_basis",
        out_shape=(
            jax.ShapeDtypeStruct((K, ROWS_DEV), jnp.float32),
            jax.ShapeDtypeStruct((K, K), jnp.float32),
        ),
        in_specs=[vmem, vmem],
        out_specs=(hbm, vmem),
        scratch_shapes=[
            pltpu.VMEM((K, ROWS_DEV), jnp.float32),
            dma((BASIS_PARTS,)),
        ],
        compiler_params=pltpu.CompilerParams(vmem_limit_bytes=8 * 1024 * 1024),
    )(gram, split)
    return (jnp.swapaxes(basis, 0, 1).reshape(1, 1, ROWS_DEV, K), factor)


def solution(mesh):
    in_specs = (
        P("gx", "gy", None, None, None, None),
        P("gx", "gy", None, None),
        P("gx", "gy", None, None),
    )
    out_specs = (P("gx", "gy", None, None), P())
    return jax.shard_map(shards, mesh=mesh, in_specs=in_specs, out_specs=out_specs, check_vma=False)
```

```python
import functools

import jax
import jax.numpy as jnp
from jax import lax
from jax.experimental import pallas as pl
from jax.experimental.pallas import tpu as pltpu
from jax.sharding import PartitionSpec as P

K = 64
TILE = 128
NB = 20
TILES = 32
ROWS_DEV = TILES * TILE
N_GX = 8
N_GY = 16
ROWS = ROWS_DEV * N_GX * N_GY
CHUNKS = 4
TURNED = 1
TURN_AT = 2
PART = TILES // CHUNKS
A_COPIES = 8
UNROLL = TILES
FOLDED = 24
MESH = pl.DeviceIdType.MESH


def slot_of(x, y):
    return (lax.rem(x, 4) * 4 + lax.rem(y, 4)) * TILES


def folded(gram):
    rows = gram[:K] + gram[K:]
    both = rows + pltpu.roll(rows, K, 1)
    lane = lax.broadcasted_iota(jnp.int32, (16, 2 * K), 1)
    top = jnp.where(lane < K, both[:16], both[16:32])
    lane = lane[:8]
    low = both[32:]
    moved = pltpu.roll(low, 32, 1)
    corner = jnp.where(
        lane < 64,
        jnp.where(lane < 32, moved[:8], low[8:16]),
        jnp.where(lane < 96, moved[16:24], low[24:]),
    )
    return jnp.concatenate([top, corner], axis=0)


def unfolded(packed):
    top, corner = packed[:16], packed[16:]
    upper = jnp.concatenate([top, pltpu.roll(top, K, 1)], axis=0)
    square = jnp.concatenate([upper, jnp.zeros((96, 2 * K), jnp.float32)], axis=0)
    left = square.T[32:64]
    right = jnp.concatenate(
        [pltpu.roll(corner, 32, 1), corner, pltpu.roll(corner, 96, 1), pltpu.roll(corner, 64, 1)], axis=0
    )
    lane = lax.broadcasted_iota(jnp.int32, (32, 2 * K), 1)
    return jnp.concatenate([upper, jnp.where(lane < 32, left, right)], axis=0)


def product_kernel(
    tiles_hbm, block_hbm, links_hbm, split, gram_ref,
    tiles, table, turned, links, across_x, across_y,
    tile_sem, own_sem, gy_send, gy_recv, near_send, near_recv, far_send, far_recv, turn_send, turn_recv,
    sx_send, sx_recv, sy_send, sy_recv, links_sem,
):
    me_x, me_y = lax.axis_index("gx"), lax.axis_index("gy")

    def ring_x(step):
        return lax.rem(me_x + step + N_GX, N_GX)

    def ring_y(step):
        return lax.rem(me_y + step + N_GY, N_GY)

    core = lax.rem(me_x, 2)
    near_x = me_x + 1 - 2 * core
    far_x = ring_x(2 * core - 1)
    own = slot_of(me_x, me_y)

    own_copy = pltpu.make_async_copy(block_hbm, turned, own_sem)
    own_copy.start()
    links_copy = pltpu.make_async_copy(links_hbm, links, links_sem)
    links_copy.start()
    barrier = pltpu.get_barrier_semaphore()

    def greet(x, y):
        pl.semaphore_signal(barrier, inc=1, device_id=(x, y), device_id_type=MESH)

    for step in sorted(range(1, N_GY), key=lambda n: min(n, N_GY - n)):
        greet(me_x, ring_y(step))
    for step in sorted(range(1, N_GX), key=lambda n: min(n, N_GX - n)):
        greet(ring_x(step), me_y)
    own_copy.wait()
    for i in range(TILES):
        table[own + i] = turned[:, i * TILE : (i + 1) * TILE]
    pl.semaphore_wait(barrier, N_GX + N_GY - 2)

    started = []

    def span(slot, part):
        return table.at[pl.ds(slot + part * PART, PART)]

    def push(slot, part, send, recv, x, y):
        copy = pltpu.make_async_remote_copy(
            src_ref=span(slot, part), dst_ref=span(slot, part), send_sem=send, recv_sem=recv,
            device_id=(x, y), device_id_type=MESH,
        )
        copy.start()
        started.append(copy)

    def landed(slot, part, sem):
        pltpu.make_async_copy(span(slot, part), span(slot, part), sem).wait()

    for part in range(CHUNKS):
        for d, step in enumerate((1, -1)):
            push(own, part, gy_send.at[d, part], gy_recv.at[d, part], me_x, ring_y(step))
        push(own, part, far_send.at[0, part], far_recv.at[0, part], far_x, me_y)
        push(own, part, near_send.at[0, part], near_recv.at[0, part], near_x, me_y)

    copies = []
    group = TILES // A_COPIES
    for i in range(A_COPIES):
        copy = pltpu.make_async_copy(
            tiles_hbm.at[pl.ds(i * group, group)], tiles.at[pl.ds(i * group, group)], tile_sem.at[i]
        )
        copy.start()
        copies.append(copy)

    early = CHUNKS - TURNED
    for part in range(CHUNKS):
        for d, step in enumerate((-1, 1)):
            slot = slot_of(me_x, ring_y(step))
            landed(slot, part, gy_recv.at[d, part])
            if part < early:
                push(slot, part, far_send.at[1 + d, part], far_recv.at[1 + d, part], far_x, me_y)
            push(slot, part, near_send.at[1 + d, part], near_recv.at[1 + d, part], near_x, me_y)
        if part == TURN_AT:
            for late in range(TURNED):
                slot = slot_of(far_x, me_y)
                landed(slot, early + late, far_recv.at[0, early + late])
                for d, step in enumerate((1, -1)):
                    push(slot, early + late, turn_send.at[d, late], turn_recv.at[d, late], me_x, ring_y(step))
    links_copy.wait()
    for copy in copies:
        copy.wait()
    for which, dy in enumerate((0, -1, 1)):
        for part in range(CHUNKS):
            landed(slot_of(near_x, ring_y(dy)), part, near_recv.at[which, part])
            if part < early:
                landed(slot_of(far_x, ring_y(dy)), part, far_recv.at[which, part])
            elif which:
                landed(slot_of(far_x, ring_y(dy)), part, turn_recv.at[which - 1, part - early])

    def row_tile(t, carry):
        near = jnp.concatenate([tiles[t, j] for j in range(NB)], axis=1)
        picked = []
        for j in range(NB):
            link = links[j, 0, t]
            picked.append(table[((link >> 2) & (12 * TILES)) | (link & (4 * TILES - 1))])
        rows = jnp.concatenate(picked, axis=1)
        image = lax.dot_general(
            near, rows, (((1,), (1,)), ((), ())), preferred_element_type=jnp.float32
        ).T
        high = image.astype(jnp.bfloat16)
        low = (image - high.astype(jnp.float32)).astype(jnp.bfloat16)
        here = pl.ds(pl.multiple_of(t * TILE, TILE), TILE)
        split[:K, here] = high
        split[K:, here] = low
        return carry

    lax.fori_loop(0, TILES, row_tile, 0, unroll=UNROLL)
    image = split[...]
    gram = lax.dot_general(image, image, (((1,), (1,)), ((), ())), preferred_element_type=jnp.float32)

    def summed(value, gathered, count, me, send, recv, device, earlier):
        gathered[me] = value
        sends = []
        for step in range(1, count):
            copy = pltpu.make_async_remote_copy(
                src_ref=gathered.at[me], dst_ref=gathered.at[me], send_sem=send.at[step], recv_sem=recv.at[step],
                device_id=device(step), device_id_type=MESH,
            )
            copy.start()
            sends.append(copy)
        for copy in earlier:
            copy.wait_send()
        for step in range(1, count):
            source = gathered.at[lax.rem(me - step + count, count)]
            pltpu.make_async_copy(source, source, recv.at[step]).wait()
        terms = [gathered[i] for i in range(count)]
        while len(terms) > 1:
            terms = [a + b for a, b in zip(terms[::2], terms[1::2])]
        return terms[0], sends

    partial, sends_x = summed(
        folded(gram), across_x, N_GX, me_x, sx_send, sx_recv, lambda step: (ring_x(step), me_y), started
    )
    total, sends_y = summed(
        partial, across_y, N_GY, me_y, sy_send, sy_recv, lambda step: (me_x, ring_y(step)), sends_x
    )
    gram_ref[...] = unfolded(total)
    for copy in sends_y:
        copy.wait_send()


def eliminated(rows):
    count = K // 8
    sub = lax.broadcasted_iota(jnp.int32, (8, 128), 0)
    zero = jnp.zeros((8, 128), jnp.float32)

    def spread(x):
        return jnp.broadcast_to(x, (8, 128))

    pivots = [zero] * count
    for first in range(0, K, PANEL):
        columns = [
            {r: spread(rows[r][:, first + j : first + j + 1]) for r in range(first // 8, count)} for j in range(PANEL)
        ]
        for j in range(PANEL):
            p, at = divmod(first + j, 8)
            pivot = spread(columns[j][p][at : at + 1])
            pivots[p] = jnp.where(sub == at, pivot, pivots[p])
            inverse = 1.0 / pivot
            pivot_row = spread(rows[p][at : at + 1])
            later = {i: spread(columns[i][p][at : at + 1]) for i in range(j + 1, PANEL)}
            for r in range(p, count):
                scaled = columns[j][r] * inverse
                if r == p:
                    scaled = jnp.where(sub > at, scaled, zero)
                for i in range(j + 1, PANEL):
                    columns[i][r] = columns[i][r] - scaled * later[i]
                rows[r] = rows[r] - scaled * pivot_row
    return rows, pivots


PANEL = 16
BASIS_PARTS = 8


def basis_kernel(gram_ref, split, basis_hbm, factor_ref, basis, sems):
    lane = lax.broadcasted_iota(jnp.int32, (8, 128), 1)
    sub = lax.broadcasted_iota(jnp.int32, (8, 128), 0)
    count = K // 8
    rows = [
        jnp.where(lane < K, gram_ref[8 * r : 8 * r + 8], jnp.where(lane - K == sub + 8 * r, 1.0, 0.0))
        for r in range(count)
    ]
    rows, pivots = eliminated(rows)
    scale = float(ROWS) ** 0.5
    highs, lows = [], []
    for r in range(count):
        root = lax.rsqrt(pivots[r])
        root = root * (1.5 - 0.5 * pivots[r] * root * root)
        upper = rows[r] * root
        factor_ref[8 * r : 8 * r + 8] = (jnp.where(lane >= sub + 8 * r, upper, 0.0) * (1.0 / scale))[:, :K]
        solve = upper * scale
        solve = jnp.where(lane < K, pltpu.roll(solve, K, 1), solve)
        high = solve.astype(jnp.bfloat16)
        highs.append(high)
        lows.append((solve - high.astype(jnp.float32)).astype(jnp.bfloat16))
    solver = jnp.concatenate(highs + lows, 0)
    width = ROWS_DEV // BASIS_PARTS
    stores = []
    for part in range(BASIS_PARTS):
        here = slice(part * width, (part + 1) * width)
        products = jnp.dot(solver, split[:, here], preferred_element_type=jnp.float32)
        basis[:, here] = products[:K] + products[K:]
        at = pl.ds(part * width, width)
        store = pltpu.make_async_copy(basis.at[:, at], basis_hbm.at[:, at], sems.at[part])
        store.start()
        stores.append(store)
    for store in stores:
        store.wait()


def shards(near_tiles, block, adjacency):
    hbm, vmem = (pl.BlockSpec(memory_space=space) for space in (pltpu.HBM, pltpu.VMEM))
    dma = pltpu.SemaphoreType.DMA
    links = jnp.transpose(adjacency, (0, 3, 1, 2)).reshape(NB, 1, TILES)
    turned = jnp.swapaxes(block[0, 0], 0, 1)
    split, gram = pl.pallas_call(
        product_kernel,
        name="near_product",
        out_shape=(
            jax.ShapeDtypeStruct((2 * K, ROWS_DEV), jnp.bfloat16),
            jax.ShapeDtypeStruct((K, 2 * K), jnp.float32),
        ),
        in_specs=[hbm, hbm, hbm],
        out_specs=(vmem, vmem),
        scratch_shapes=[
            pltpu.VMEM((TILES, NB, TILE, TILE), jnp.bfloat16),
            pltpu.VMEM((16 * TILES, K, TILE), jnp.bfloat16),
            pltpu.VMEM((K, ROWS_DEV), jnp.bfloat16),
            pltpu.SMEM((NB, 1, TILES), jnp.int32),
            pltpu.VMEM((N_GX, FOLDED, 2 * K), jnp.float32),
            pltpu.VMEM((N_GY, FOLDED, 2 * K), jnp.float32),
            dma((A_COPIES,)),
            dma,
            dma((2, CHUNKS)),
            dma((2, CHUNKS)),
            dma((3, CHUNKS)),
            dma((3, CHUNKS)),
            dma((3, CHUNKS)),
            dma((3, CHUNKS)),
            dma((2, TURNED)),
            dma((2, TURNED)),
            dma((N_GX,)),
            dma((N_GX,)),
            dma((N_GY,)),
            dma((N_GY,)),
            dma,
        ],
        compiler_params=pltpu.CompilerParams(
            collective_id=0, has_side_effects=True, vmem_limit_bytes=40 * 1024 * 1024
        ),
    )(near_tiles[0, 0], *(pltpu.with_memory_space_constraint(x, pltpu.HBM) for x in (turned, links)))
    basis, factor = pl.pallas_call(
        basis_kernel,
        name="orthonormal_basis",
        out_shape=(
            jax.ShapeDtypeStruct((K, ROWS_DEV), jnp.float32),
            jax.ShapeDtypeStruct((K, K), jnp.float32),
        ),
        in_specs=[vmem, vmem],
        out_specs=(hbm, vmem),
        scratch_shapes=[
            pltpu.VMEM((K, ROWS_DEV), jnp.float32),
            dma((BASIS_PARTS,)),
        ],
        compiler_params=pltpu.CompilerParams(vmem_limit_bytes=8 * 1024 * 1024),
    )(gram, split)
    return (jnp.swapaxes(basis, 0, 1).reshape(1, 1, ROWS_DEV, K), factor)


def solution(mesh):
    in_specs = (
        P("gx", "gy", None, None, None, None),
        P("gx", "gy", None, None),
        P("gx", "gy", None, None),
    )
    out_specs = (P("gx", "gy", None, None), P())
    return jax.shard_map(shards, mesh=mesh, in_specs=in_specs, out_specs=out_specs, check_vma=False)
```

```python
import functools

import jax
import jax.numpy as jnp
from jax import lax
from jax.experimental import pallas as pl
from jax.experimental.pallas import tpu as pltpu
from jax.sharding import PartitionSpec as P

K = 64
TILE = 128
NB = 20
TILES = 32
ROWS_DEV = TILES * TILE
N_GX = 8
N_GY = 16
ROWS = ROWS_DEV * N_GX * N_GY
CHUNKS = 4
TURNED = 1
TURN_AT = 1
PART = TILES // CHUNKS
A_COPIES = 8
UNROLL = TILES
FOLDED = 24
MESH = pl.DeviceIdType.MESH


def slot_of(x, y):
    return (lax.rem(x, 4) * 4 + lax.rem(y, 4)) * TILES


def folded(gram):
    rows = gram[:K] + gram[K:]
    both = rows + pltpu.roll(rows, K, 1)
    lane = lax.broadcasted_iota(jnp.int32, (16, 2 * K), 1)
    top = jnp.where(lane < K, both[:16], both[16:32])
    lane = lane[:8]
    low = both[32:]
    moved = pltpu.roll(low, 32, 1)
    corner = jnp.where(
        lane < 64,
        jnp.where(lane < 32, moved[:8], low[8:16]),
        jnp.where(lane < 96, moved[16:24], low[24:]),
    )
    return jnp.concatenate([top, corner], axis=0)


def unfolded(packed):
    top, corner = packed[:16], packed[16:]
    upper = jnp.concatenate([top, pltpu.roll(top, K, 1)], axis=0)
    square = jnp.concatenate([upper, jnp.zeros((96, 2 * K), jnp.float32)], axis=0)
    left = square.T[32:64]
    right = jnp.concatenate(
        [pltpu.roll(corner, 32, 1), corner, pltpu.roll(corner, 96, 1), pltpu.roll(corner, 64, 1)], axis=0
    )
    lane = lax.broadcasted_iota(jnp.int32, (32, 2 * K), 1)
    return jnp.concatenate([upper, jnp.where(lane < 32, left, right)], axis=0)


def product_kernel(
    tiles_hbm, block_hbm, links_hbm, split, gram_ref,
    tiles, table, turned, links, across_x, across_y,
    tile_sem, own_sem, gy_send, gy_recv, near_send, near_recv, far_send, far_recv, turn_send, turn_recv,
    sx_send, sx_recv, sy_send, sy_recv, links_sem,
):
    me_x, me_y = lax.axis_index("gx"), lax.axis_index("gy")

    def ring_x(step):
        return lax.rem(me_x + step + N_GX, N_GX)

    def ring_y(step):
        return lax.rem(me_y + step + N_GY, N_GY)

    core = lax.rem(me_x, 2)
    near_x = me_x + 1 - 2 * core
    far_x = ring_x(2 * core - 1)
    own = slot_of(me_x, me_y)

    own_copy = pltpu.make_async_copy(block_hbm, turned, own_sem)
    own_copy.start()
    links_copy = pltpu.make_async_copy(links_hbm, links, links_sem)
    links_copy.start()
    barrier = pltpu.get_barrier_semaphore()

    def greet(x, y):
        pl.semaphore_signal(barrier, inc=1, device_id=(x, y), device_id_type=MESH)

    for step in sorted(range(1, N_GY), key=lambda n: min(n, N_GY - n)):
        greet(me_x, ring_y(step))
    for step in sorted(range(1, N_GX), key=lambda n: min(n, N_GX - n)):
        greet(ring_x(step), me_y)
    own_copy.wait()
    for i in range(TILES):
        table[own + i] = turned[:, i * TILE : (i + 1) * TILE]
    pl.semaphore_wait(barrier, N_GX + N_GY - 2)

    started = []

    def span(slot, part):
        return table.at[pl.ds(slot + part * PART, PART)]

    def push(slot, part, send, recv, x, y):
        copy = pltpu.make_async_remote_copy(
            src_ref=span(slot, part), dst_ref=span(slot, part), send_sem=send, recv_sem=recv,
            device_id=(x, y), device_id_type=MESH,
        )
        copy.start()
        started.append(copy)

    def landed(slot, part, sem):
        pltpu.make_async_copy(span(slot, part), span(slot, part), sem).wait()

    for part in range(CHUNKS):
        for d, step in enumerate((1, -1)):
            push(own, part, gy_send.at[d, part], gy_recv.at[d, part], me_x, ring_y(step))
        push(own, part, far_send.at[0, part], far_recv.at[0, part], far_x, me_y)
        push(own, part, near_send.at[0, part], near_recv.at[0, part], near_x, me_y)

    copies = []
    group = TILES // A_COPIES
    for i in range(A_COPIES):
        copy = pltpu.make_async_copy(
            tiles_hbm.at[pl.ds(i * group, group)], tiles.at[pl.ds(i * group, group)], tile_sem.at[i]
        )
        copy.start()
        copies.append(copy)

    early = CHUNKS - TURNED
    for part in range(CHUNKS):
        for d, step in enumerate((-1, 1)):
            slot = slot_of(me_x, ring_y(step))
            landed(slot, part, gy_recv.at[d, part])
            if part < early:
                push(slot, part, far_send.at[1 + d, part], far_recv.at[1 + d, part], far_x, me_y)
            push(slot, part, near_send.at[1 + d, part], near_recv.at[1 + d, part], near_x, me_y)
        if part == TURN_AT:
            for late in range(TURNED):
                slot = slot_of(far_x, me_y)
                landed(slot, early + late, far_recv.at[0, early + late])
                for d, step in enumerate((1, -1)):
                    push(slot, early + late, turn_send.at[d, late], turn_recv.at[d, late], me_x, ring_y(step))
    links_copy.wait()
    for copy in copies:
        copy.wait()
    for which, dy in enumerate((0, -1, 1)):
        for part in range(CHUNKS):
            landed(slot_of(near_x, ring_y(dy)), part, near_recv.at[which, part])
            if part < early:
                landed(slot_of(far_x, ring_y(dy)), part, far_recv.at[which, part])
            elif which:
                landed(slot_of(far_x, ring_y(dy)), part, turn_recv.at[which - 1, part - early])

    def row_tile(t, carry):
        near = jnp.concatenate([tiles[t, j] for j in range(NB)], axis=1)
        picked = []
        for j in range(NB):
            link = links[j, 0, t]
            picked.append(table[((link >> 2) & (12 * TILES)) | (link & (4 * TILES - 1))])
        rows = jnp.concatenate(picked, axis=1)
        image = lax.dot_general(
            near, rows, (((1,), (1,)), ((), ())), preferred_element_type=jnp.float32
        ).T
        high = image.astype(jnp.bfloat16)
        low = (image - high.astype(jnp.float32)).astype(jnp.bfloat16)
        here = pl.ds(pl.multiple_of(t * TILE, TILE), TILE)
        split[:K, here] = high
        split[K:, here] = low
        return carry

    lax.fori_loop(0, TILES, row_tile, 0, unroll=UNROLL)
    image = split[...]
    gram = lax.dot_general(image, image, (((1,), (1,)), ((), ())), preferred_element_type=jnp.float32)

    def summed(value, gathered, count, me, send, recv, device, earlier):
        gathered[me] = value
        sends = []
        for step in range(1, count):
            copy = pltpu.make_async_remote_copy(
                src_ref=gathered.at[me], dst_ref=gathered.at[me], send_sem=send.at[step], recv_sem=recv.at[step],
                device_id=device(step), device_id_type=MESH,
            )
            copy.start()
            sends.append(copy)
        for copy in earlier:
            copy.wait_send()
        for step in range(1, count):
            source = gathered.at[lax.rem(me - step + count, count)]
            pltpu.make_async_copy(source, source, recv.at[step]).wait()
        terms = [gathered[i] for i in range(count)]
        while len(terms) > 1:
            terms = [a + b for a, b in zip(terms[::2], terms[1::2])]
        return terms[0], sends

    partial, sends_x = summed(
        folded(gram), across_x, N_GX, me_x, sx_send, sx_recv, lambda step: (ring_x(step), me_y), started
    )
    total, sends_y = summed(
        partial, across_y, N_GY, me_y, sy_send, sy_recv, lambda step: (me_x, ring_y(step)), sends_x
    )
    gram_ref[...] = unfolded(total)
    for copy in sends_y:
        copy.wait_send()


def eliminated(rows):
    count = K // 8
    sub = lax.broadcasted_iota(jnp.int32, (8, 128), 0)
    zero = jnp.zeros((8, 128), jnp.float32)

    def spread(x):
        return jnp.broadcast_to(x, (8, 128))

    pivots = [zero] * count
    for first in range(0, K, PANEL):
        columns = [
            {r: spread(rows[r][:, first + j : first + j + 1]) for r in range(first // 8, count)} for j in range(PANEL)
        ]
        for j in range(PANEL):
            p, at = divmod(first + j, 8)
            pivot = spread(columns[j][p][at : at + 1])
            pivots[p] = jnp.where(sub == at, pivot, pivots[p])
            inverse = 1.0 / pivot
            pivot_row = spread(rows[p][at : at + 1])
            later = {i: spread(columns[i][p][at : at + 1]) for i in range(j + 1, PANEL)}
            for r in range(p, count):
                scaled = columns[j][r] * inverse
                if r == p:
                    scaled = jnp.where(sub > at, scaled, zero)
                for i in range(j + 1, PANEL):
                    columns[i][r] = columns[i][r] - scaled * later[i]
                rows[r] = rows[r] - scaled * pivot_row
    return rows, pivots


PANEL = 16
BASIS_PARTS = 8


def basis_kernel(gram_ref, split, basis_hbm, factor_ref, basis, sems):
    lane = lax.broadcasted_iota(jnp.int32, (8, 128), 1)
    sub = lax.broadcasted_iota(jnp.int32, (8, 128), 0)
    count = K // 8
    rows = [
        jnp.where(lane < K, gram_ref[8 * r : 8 * r + 8], jnp.where(lane - K == sub + 8 * r, 1.0, 0.0))
        for r in range(count)
    ]
    rows, pivots = eliminated(rows)
    scale = float(ROWS) ** 0.5
    highs, lows = [], []
    for r in range(count):
        root = lax.rsqrt(pivots[r])
        root = root * (1.5 - 0.5 * pivots[r] * root * root)
        upper = rows[r] * root
        factor_ref[8 * r : 8 * r + 8] = (jnp.where(lane >= sub + 8 * r, upper, 0.0) * (1.0 / scale))[:, :K]
        solve = upper * scale
        solve = jnp.where(lane < K, pltpu.roll(solve, K, 1), solve)
        high = solve.astype(jnp.bfloat16)
        highs.append(high)
        lows.append((solve - high.astype(jnp.float32)).astype(jnp.bfloat16))
    solver = jnp.concatenate(highs + lows, 0)
    width = ROWS_DEV // BASIS_PARTS
    stores = []
    for part in range(BASIS_PARTS):
        here = slice(part * width, (part + 1) * width)
        products = jnp.dot(solver, split[:, here], preferred_element_type=jnp.float32)
        basis[:, here] = products[:K] + products[K:]
        at = pl.ds(part * width, width)
        store = pltpu.make_async_copy(basis.at[:, at], basis_hbm.at[:, at], sems.at[part])
        store.start()
        stores.append(store)
    for store in stores:
        store.wait()


def shards(near_tiles, block, adjacency):
    hbm, vmem = (pl.BlockSpec(memory_space=space) for space in (pltpu.HBM, pltpu.VMEM))
    dma = pltpu.SemaphoreType.DMA
    links = jnp.transpose(adjacency, (0, 3, 1, 2)).reshape(NB, 1, TILES)
    turned = jnp.swapaxes(block[0, 0], 0, 1)
    split, gram = pl.pallas_call(
        product_kernel,
        name="near_product",
        out_shape=(
            jax.ShapeDtypeStruct((2 * K, ROWS_DEV), jnp.bfloat16),
            jax.ShapeDtypeStruct((K, 2 * K), jnp.float32),
        ),
        in_specs=[hbm, hbm, hbm],
        out_specs=(vmem, vmem),
        scratch_shapes=[
            pltpu.VMEM((TILES, NB, TILE, TILE), jnp.bfloat16),
            pltpu.VMEM((16 * TILES, K, TILE), jnp.bfloat16),
            pltpu.VMEM((K, ROWS_DEV), jnp.bfloat16),
            pltpu.SMEM((NB, 1, TILES), jnp.int32),
            pltpu.VMEM((N_GX, FOLDED, 2 * K), jnp.float32),
            pltpu.VMEM((N_GY, FOLDED, 2 * K), jnp.float32),
            dma((A_COPIES,)),
            dma,
            dma((2, CHUNKS)),
            dma((2, CHUNKS)),
            dma((3, CHUNKS)),
            dma((3, CHUNKS)),
            dma((3, CHUNKS)),
            dma((3, CHUNKS)),
            dma((2, TURNED)),
            dma((2, TURNED)),
            dma((N_GX,)),
            dma((N_GX,)),
            dma((N_GY,)),
            dma((N_GY,)),
            dma,
        ],
        compiler_params=pltpu.CompilerParams(
            collective_id=0, has_side_effects=True, vmem_limit_bytes=40 * 1024 * 1024
        ),
    )(near_tiles[0, 0], *(pltpu.with_memory_space_constraint(x, pltpu.HBM) for x in (turned, links)))
    basis, factor = pl.pallas_call(
        basis_kernel,
        name="orthonormal_basis",
        out_shape=(
            jax.ShapeDtypeStruct((K, ROWS_DEV), jnp.float32),
            jax.ShapeDtypeStruct((K, K), jnp.float32),
        ),
        in_specs=[vmem, vmem],
        out_specs=(hbm, vmem),
        scratch_shapes=[
            pltpu.VMEM((K, ROWS_DEV), jnp.float32),
            dma((BASIS_PARTS,)),
        ],
        compiler_params=pltpu.CompilerParams(vmem_limit_bytes=8 * 1024 * 1024),
    )(gram, split)
    return (jnp.swapaxes(basis, 0, 1).reshape(1, 1, ROWS_DEV, K), factor)


def solution(mesh):
    in_specs = (
        P("gx", "gy", None, None, None, None),
        P("gx", "gy", None, None),
        P("gx", "gy", None, None),
    )
    out_specs = (P("gx", "gy", None, None), P())
    return jax.shard_map(shards, mesh=mesh, in_specs=in_specs, out_specs=out_specs, check_vma=False)
```
